512 devices in a mesh: section: 2 (over core), expert: 64 (over y, z), tp: 4 (over x).
Axes of the slice: x: 4, y: 4, z: 16, core: 2. Of those that a mesh axis runs over, the one named last changes fastest.
Arguments:
- tokens: bfloat16 [8192, 4096], P('expert', ('tp', 'section')), may hold values from -6 to 6
- out_grad: bfloat16 [8192, 4096], P('expert', ('tp', 'section')), may hold values from -12 to 12
- expert_ids: int32 [8192, 8], P('expert'), may hold values from 0 to 63, all different within a row; in each aligned block of 128 rows (0 to 127, 128 to 255, ...) at most 18 rows name the same one
- combine: float32 [8192, 8], P('expert'), may hold values from 0.05 to 0.5
- w_gate: bfloat16 [64, 4096, 768], P('expert', 'tp', 'section'), may hold values from -0.09375 to 0.09375
- w_up: bfloat16 [64, 4096, 768], P('expert', 'tp', 'section'), may hold values from -0.09375 to 0.09375
- w_down: bfloat16 [64, 768, 4096], P('expert', 'section', 'tp'), may hold values from -0.21875 to 0.21875
Outputs:
- token_grad: bfloat16 [8192, 4096], P('expert', ('tp', 'section'))
- gate_weight_grad: bfloat16 [64, 4096, 768], P('expert', 'tp', 'section')
- up_weight_grad: bfloat16 [64, 4096, 768], P('expert', 'tp', 'section')
- down_weight_grad: bfloat16 [64, 768, 4096], P('expert', 'section', 'tp')
The draws below stay inside these ranges and needn't reach their ends.
Inputs may be any that keep to these rules, and one draw needn't show every extreme that they name: `expert_ids`: each row names 8 different experts; among the 128 rows of one index of expert no expert is named more than 18 times, a bound that some block reaches.
All inputs are finite; a program needn't handle non-finite values.
Results may differ from the reference program's by a relative error of at most 0.025.
Values may be sent and summed in bfloat16 or wider, within the bound.
No kernel may reach another device: no remote copies, remote signals or barrier semaphores. Data moves between devices by JAX's collectives and lax.ppermute only.
A program may use at most 64 MiB of HBM per device.

```python
import math
import jax
import jax.numpy as jnp
import numpy as np
from jax import lax

D = 4096
FF = 768
TOK_DEV = 128
EXPERTS = 64
TOP = 8
CAP = 18
TOKENS = 8192
N_SECTION = 2
N_EXPERT = 64
N_TP = 4


def block_scale(key, extent, shards, least, high):
    def one(position, parts):
        steps = jax.random.uniform(jax.random.fold_in(jax.random.fold_in(key, 6), position), (parts,), jnp.float32, least / len(shards), high / len(shards))
        return jnp.repeat(jnp.exp(steps), extent[position] // parts).reshape((-1,) + (1,) * (len(extent) - position - 1))

    loudness = one(*shards[0])
    for cut in shards[1:]:
        loudness = loudness * one(*cut)
    return loudness


def routed_block(rng, own, number, rows, count, top, reach, slope):
    sequence = jax.random.permutation(rng, count)
    heavy_load, usual = load_shares(count, rows * top, reach, slope, True), load_shares(count, rows * top, reach, slope, False)
    places = jnp.arange(count)

    def named(tallies, turn):
        used = int((tallies > 0).sum())
        fixed = max(1, used // 4)
        moved = fixed + (places - fixed + turn * (used - fixed)) % max(1, count - fixed)
        return jnp.zeros((count,), jnp.int32).at[sequence[jnp.where(places < fixed, places, moved)]].set(jnp.asarray(tallies, jnp.int32))

    tallies = jnp.where(number % 4 == 0, named(heavy_load, number // 4), named(usual, number - number // 4 - 1))
    mixed = jax.random.permutation(jax.random.fold_in(own, 3), count)
    giver, receiver = mixed[0:count // 2 * 2:2], mixed[1:count // 2 * 2:2]
    room = jnp.minimum(tallies[giver] - 1, reach - tallies[receiver]) // 2
    room = jnp.where((giver == sequence[0]) | (receiver == sequence[0]) | (tallies[receiver] == 0), 0, jnp.maximum(room, 0))
    moved = jax.random.randint(jax.random.fold_in(own, 4), (count // 2,), 0, 1 << 20) % (room + 1)
    tallies = tallies.at[giver].add(-moved).at[receiver].add(moved)
    labels = jnp.searchsorted(jnp.cumsum(tallies), jnp.arange(rows * top), side="right").astype(jnp.int32)
    grid = labels.reshape(top, rows).T
    grid = grid[jax.random.permutation(jax.random.fold_in(own, 1), rows)]
    turn = jax.random.randint(jax.random.fold_in(own, 2), (rows, 1), 0, top)
    return jnp.take_along_axis(grid, (jnp.arange(top)[None, :] + turn) % top, axis=1)


def load_shares(amount, total, most, slope, full):
    weights = [(1 << 20) // math.isqrt(grade ** slope) + 1 for grade in range(1, amount + 1)]
    largest = most if full else min(most, max(-(-total // amount), total * weights[0] // sum(weights)))
    least = 1 if total - largest >= amount - 1 else 0
    holding, surplus = [largest] + [least] * (amount - 1), total - largest - least * (amount - 1)
    while surplus > 0:
        free = [i for i in range(1, amount) if holding[i] < largest] or [i for i in range(1, amount) if holding[i] < most]
        mass, remaining = sum([weights[i] for i in free]), surplus
        for i in free:
            extra = min(most - holding[i], max(1, remaining * weights[i] // mass), surplus)
            holding[i] = holding[i] + extra
            surplus = surplus - extra
    return np.array(holding)


def scatter_about(stream_key, extent, width, limit, shards=(), kind=jnp.bfloat16):
    drawn = jax.random.normal(stream_key, extent, jnp.float32) * width
    if len(shards) > 0:
        drawn = block_scale(stream_key, extent, shards, -0.22, 0.18) * drawn
    return jnp.clip(drawn, min=-limit, max=limit).astype(kind)


def setup_inputs(seed: int = 0) -> dict:
    keys = jax.random.split(jax.random.key(seed), 8)
    tokens = scatter_about(keys[0], (TOKENS, D), 1.0, 6.0, ((0, 64), (1, 8)))
    out_grad = scatter_about(keys[1], (TOKENS, D), 2.0, 12.0, ((0, 64), (1, 8)))
    expert_ids_keys = jax.random.split(jax.random.fold_in(keys[2], 1), TOKENS // TOK_DEV)
    expert_ids_turns = jax.random.permutation(jax.random.fold_in(keys[2], 3), TOKENS // TOK_DEV)
    expert_ids = jax.vmap(lambda own, number: routed_block(jax.random.fold_in(keys[2], 2), own, number, TOK_DEV, EXPERTS, TOP, CAP, 2))(expert_ids_keys, expert_ids_turns).reshape((TOKENS, TOP))
    combine = jnp.clip(jnp.exp(math.log(0.5) - 2.3025851 * jax.random.uniform(keys[3], (TOKENS, TOP), jnp.float32) ** block_scale(keys[3], (TOKENS, TOP), ((0, 64),), -0.2, 0.2)), 0.05, 0.5)
    w_gate = scatter_about(keys[4], (EXPERTS, D, FF), D ** -0.5, 0.09375, ((0, 64), (1, 4), (2, 2)))
    w_up = scatter_about(keys[5], (EXPERTS, D, FF), D ** -0.5, 0.09375, ((0, 64), (1, 4), (2, 2)))
    w_down = scatter_about(keys[6], (EXPERTS, FF, D), FF ** -0.5, 0.21875, ((0, 64), (1, 2), (2, 4)))
    return {"tokens": tokens, "out_grad": out_grad, "expert_ids": expert_ids, "combine": combine, "w_gate": w_gate, "w_up": w_up, "w_down": w_down}


def block_slots(block_ids):
    flat_ids = block_ids.reshape(-1)
    pick_count = flat_ids.shape[0]
    onehot = (flat_ids[:, None] == jnp.arange(EXPERTS, dtype=jnp.int32)[None, :]).astype(jnp.int32)
    earlier = jnp.cumsum(onehot, axis=0) - onehot
    slot_index = jnp.sum(earlier * onehot, axis=1)
    place_index = flat_ids * CAP + slot_index
    source = jnp.zeros((EXPERTS * CAP,), jnp.int32).at[place_index].set(jnp.arange(pick_count, dtype=jnp.int32))
    filled = jnp.zeros((EXPERTS * CAP,), jnp.int32).at[place_index].set(jnp.ones((pick_count,), jnp.int32))
    return source.reshape(EXPERTS, CAP), filled.reshape(EXPERTS, CAP)


def round_back(values):
    return lax.optimization_barrier(values.astype(jnp.bfloat16)).astype(jnp.float32)


def reference(tokens, out_grad, expert_ids, combine, w_gate, w_up, w_down):
    sources, filled = jax.vmap(block_slots)(expert_ids.reshape(N_EXPERT, TOK_DEV, TOP))
    offsets = (jnp.arange(N_EXPERT, dtype=jnp.int32) * (TOK_DEV * TOP))[:, None]
    flat_weights = combine.reshape(-1)
    quarter = D // N_TP
    half_ff = FF // N_SECTION
    rows_total = N_EXPERT * CAP

    def one_expert(total_grad, expert):
        picks = (sources[:, expert, :] + offsets).reshape(-1)
        live_slot = filled[:, expert, :].reshape(-1)
        token_index = picks // TOP
        keep_mask = (live_slot > 0)[:, None]
        rows_in = jnp.where(keep_mask, tokens[token_index], jnp.zeros((), jnp.bfloat16))
        scaled = out_grad[token_index].astype(jnp.float32) * flat_weights[picks][:, None]
        grad_in = jnp.where(keep_mask, scaled, jnp.zeros((), jnp.float32)).astype(jnp.bfloat16)
        gate_w = w_gate[expert]
        up_w = w_up[expert]
        down_w = w_down[expert]
        rows_q = rows_in.astype(jnp.float32).reshape(rows_total, N_TP, quarter)
        grad_q = grad_in.astype(jnp.float32).reshape(rows_total, N_TP, quarter)
        gate_pre = jnp.sum(round_back(jnp.einsum("rqd,qdf->qrf", rows_q, gate_w.astype(jnp.float32).reshape(N_TP, quarter, FF))), axis=0)
        up_pre = jnp.sum(round_back(jnp.einsum("rqd,qdf->qrf", rows_q, up_w.astype(jnp.float32).reshape(N_TP, quarter, FF))), axis=0)
        hidden_grad = jnp.sum(round_back(jnp.einsum("rqd,fqd->qrf", grad_q, down_w.astype(jnp.float32).reshape(FF, N_TP, quarter))), axis=0)
        sigmoid_g = jax.nn.sigmoid(gate_pre)
        activated = (gate_pre * sigmoid_g * up_pre).astype(jnp.bfloat16)
        gate_grad = (hidden_grad * up_pre * sigmoid_g * (1.0 + gate_pre * (1.0 - sigmoid_g))).astype(jnp.bfloat16)
        up_grad = (hidden_grad * gate_pre * sigmoid_g).astype(jnp.bfloat16)
        down_wgrad = jnp.dot(activated.T, grad_in, preferred_element_type=jnp.float32).astype(jnp.bfloat16)
        gate_wgrad = jnp.dot(rows_in.T, gate_grad, preferred_element_type=jnp.float32).astype(jnp.bfloat16)
        up_wgrad = jnp.dot(rows_in.T, up_grad, preferred_element_type=jnp.float32).astype(jnp.bfloat16)
        row_grad = jnp.zeros((rows_total, D), jnp.float32)
        for index in range(N_SECTION):
            low = index * half_ff
            high = low + half_ff
            half_part = jnp.dot(gate_grad[:, low:high], gate_w[:, low:high].T, preferred_element_type=jnp.float32)
            half_part = half_part + jnp.dot(up_grad[:, low:high], up_w[:, low:high].T, preferred_element_type=jnp.float32)
            row_grad = row_grad + round_back(half_part)
        row_grad = jnp.where(keep_mask, row_grad, jnp.zeros((), jnp.float32))
        total_grad = total_grad.at[token_index].add(row_grad)
        return total_grad, (gate_wgrad, up_wgrad, down_wgrad)

    total_grad, stacked = lax.scan(one_expert, jnp.zeros((TOKENS, D), jnp.float32), jnp.arange(EXPERTS, dtype=jnp.int32))
    return total_grad.astype(jnp.bfloat16), stacked[0], stacked[1], stacked[2]
```

```python
import functools

import jax
import jax.numpy as jnp
from jax import lax
from jax.experimental import pallas as pl
from jax.experimental.pallas import tpu as pltpu
from jax.sharding import Mesh
from jax.sharding import PartitionSpec as P

BF16 = jnp.bfloat16
F32 = jnp.float32
LANES = 128
VMEM_LIMIT = 48 << 20


def params():
    return pltpu.CompilerParams(vmem_limit_bytes=VMEM_LIMIT)


def iota(shape, dim):
    return lax.broadcasted_iota(jnp.int32, shape, dim)


def select_kernel(groups, n_y, scaled, *refs):
    pick_ref, rows_ref = refs[:2]
    out_ref = refs[-1]
    span = rows_ref.shape[0] // groups
    part = pick_ref.shape[1] // n_y
    pieces = []
    for g in range(groups):
        got = jnp.dot(
            pick_ref[g], rows_ref[g * span : (g + 1) * span, :], preferred_element_type=F32
        )
        if scaled:
            got = got * refs[2][g]
        pieces.append(got)
    for j in range(n_y):
        whole = jnp.concatenate([p[j * part : (j + 1) * part] for p in pieces], axis=0)
        out_ref[j] = whole.astype(BF16)


def select_rows(pick, rows, first, width, n_y, scale=None):
    groups, picked, span = pick.shape
    block = 256
    base = first // block
    slots = groups * picked // n_y
    in_specs = [
        pl.BlockSpec((groups, picked, span), lambda i: (0, 0, 0)),
        pl.BlockSpec((groups * span, block), lambda i: (0, base + i)),
    ]
    args = [pick, rows]
    if scale is not None:
        in_specs.append(pl.BlockSpec((groups, picked, 1), lambda i: (0, 0, 0)))
        args.append(scale)
    return pl.pallas_call(
        functools.partial(select_kernel, groups, n_y, scale is not None),
        grid=(width // block,),
        in_specs=in_specs,
        out_specs=pl.BlockSpec((n_y, slots, block), lambda i: (0, 0, i)),
        out_shape=jax.ShapeDtypeStruct((n_y, slots, width), BF16),
        compiler_params=params(),
        name="select_rows",
    )(*args)


def pair_kernel(a_ref, b_ref, wa_ref, wb_ref, out_ref):
    total = jnp.dot(a_ref[0], wa_ref[...], preferred_element_type=F32)
    total = total + jnp.dot(b_ref[0], wb_ref[...], preferred_element_type=F32)
    out_ref[0] = total.astype(BF16)


def pair_matmul(a, b, wa, wb):
    parts, rows, depth = a.shape
    width = wa.shape[1]
    row_spec = pl.BlockSpec((1, rows, depth), lambda i: (i, 0, 0))
    weight_spec = pl.BlockSpec((depth, width), lambda i: (0, 0))
    return pl.pallas_call(
        pair_kernel,
        grid=(parts,),
        in_specs=[row_spec, row_spec, weight_spec, weight_spec],
        out_specs=pl.BlockSpec((1, rows, width), lambda i: (i, 0, 0)),
        out_shape=jax.ShapeDtypeStruct((parts, rows, width), BF16),
        compiler_params=params(),
        name="pair_matmul",
    )(a, b, wa, wb)


def pack_kernel(group, mine_ref, other_ref, order_ref, out_ref):
    rows = mine_ref.shape[0]
    columns = mine_ref.shape[1] // LANES
    total = mine_ref[...] + other_ref[...].astype(F32)
    for start in range(0, rows, group):
        piece = total[start : start + group]
        stacked = jnp.concatenate(
            [piece[:, q * LANES : (q + 1) * LANES] for q in range(columns)], axis=0
        )
        packed = jnp.dot(order_ref[...], stacked.astype(BF16), preferred_element_type=F32)
        out_ref[start * columns : (start + group) * columns, :] = packed.astype(BF16)


def pack_rows(mine, other, capacity):
    rows, width = mine.shape
    columns = width // LANES
    group = 4 * capacity
    size = group * columns
    to = iota((size, size), 0)
    frm = iota((size, size), 1)
    b, q, c = to // (columns * capacity), (to // capacity) % columns, to % capacity
    order = (frm == q * group + b * capacity + c).astype(BF16)
    steps = 4
    return pl.pallas_call(
        functools.partial(pack_kernel, group),
        grid=(steps,),
        in_specs=[
            pl.BlockSpec((rows // steps, width), lambda i: (i, 0)),
            pl.BlockSpec((rows // steps, width), lambda i: (i, 0)),
            pl.BlockSpec((size, size), lambda i: (0, 0)),
        ],
        out_specs=pl.BlockSpec((rows * columns // steps, LANES), lambda i: (i, 0)),
        out_shape=jax.ShapeDtypeStruct((rows * columns, LANES), BF16),
        compiler_params=params(),
        name="pack_rows",
    )(mine, other, order)


def combine_kernel(pick_ref, rows_ref, out_ref):
    out_ref[...] = jnp.dot(pick_ref[0], rows_ref[...], preferred_element_type=F32).astype(BF16)


def combine_rows(pick, rows):
    columns, tok, depth = pick.shape
    return pl.pallas_call(
        combine_kernel,
        grid=(columns,),
        in_specs=[
            pl.BlockSpec((1, tok, depth), lambda i: (i, 0, 0)),
            pl.BlockSpec((depth, LANES), lambda i: (0, 0)),
        ],
        out_specs=pl.BlockSpec((tok, LANES), lambda i: (0, i)),
        out_shape=jax.ShapeDtypeStruct((tok, columns * LANES), BF16),
        compiler_params=params(),
        name="combine_rows",
    )(pick, rows)


def places(ids_t, combine_t, names):
    tok = ids_t.shape[1]
    hit = ids_t[None, :, :] == names[:, None, None]
    mask = jnp.any(hit, axis=1)
    weight = jnp.sum(jnp.where(hit, combine_t[None, :, :], 0.0), axis=1)
    earlier = (iota((tok, tok), 0) < iota((tok, tok), 1)).astype(BF16)
    rank = jnp.dot(mask.astype(BF16), earlier, preferred_element_type=F32)
    return jnp.where(mask, rank, -1.0), weight


def contract_rows(left, right):
    return lax.dot_general(left, right, (((0,), (0,)), ((), ())), preferred_element_type=F32)


def on_device(tokens, out_grad, expert_ids, combine, w_gate, w_up, w_down):
    tok, top = expert_ids.shape
    n_y, n_z = lax.axis_size("y"), lax.axis_size("z")
    n_tp = lax.axis_size("tp")
    experts = n_y * n_z
    capacity = (tok * top * 9 + 8 * experts - 1) // (8 * experts)
    half = tokens.shape[1]
    columns = half // LANES
    group = 4
    groups = n_z // group
    rows = experts * capacity
    section = lax.axis_index("section")
    swap = [(0, 1), (1, 0)]

    payload = jnp.concatenate([tokens, out_grad], axis=1)
    gathered = lax.all_gather(payload, "z", axis=0, tiled=True)

    both = jnp.concatenate([w_gate[0], w_up[0]], axis=1)
    hidden = w_gate.shape[2]
    down_t = w_down[0].T
    both_mine = lax.dynamic_slice_in_dim(both, section * half, half, 0)
    both_other = lax.dynamic_slice_in_dim(both, (1 - section) * half, half, 0)
    down_mine = lax.dynamic_slice_in_dim(down_t, section * half, half, 0)
    down_other = lax.dynamic_slice_in_dim(down_t, (1 - section) * half, half, 0)
    back_mine, back_other = both_mine.T, both_other.T

    ids_t, combine_t = expert_ids.T, combine.T
    line = jnp.arange(n_z * 2 * n_y, dtype=jnp.int32)
    turn = line % (2 * n_y)
    code, weight = places(ids_t, combine_t, (turn % n_y) * n_z + line // (2 * n_y))
    notice = jnp.where((turn < n_y)[:, None], code, weight).reshape(n_z, 2 * n_y, tok)
    noticed = lax.all_to_all(notice, "z", 0, 0, tiled=True)
    code_z = noticed[:, :n_y].reshape(groups, group * n_y, tok)
    weight_z = noticed[:, n_y:].reshape(groups, group * n_y, tok)
    picked = n_y * group * capacity
    place = iota((picked, group * n_y), 0)
    source = iota((picked, group * n_y), 1)
    block_of = (place // capacity) % group
    spread = (source == block_of * n_y + place // (group * capacity)).astype(BF16)
    wide_code = jnp.einsum(
        "rs,gst->grt",
        spread,
        jnp.concatenate([code_z] * group, axis=2).astype(BF16),
        preferred_element_type=F32,
    )
    spot = iota((picked, group * tok), 0)
    column = iota((picked, group * tok), 1)
    slot_f = (spot % capacity).astype(F32)
    same = (spot // capacity) % group == column // tok
    pick = jnp.logical_and(wide_code == slot_f[None], same[None]).astype(BF16)
    wide_weight = jnp.einsum(
        "rs,gst->grt",
        spread.astype(F32),
        weight_z,
        preferred_element_type=F32,
        precision=lax.Precision.HIGHEST,
    )
    scale = jnp.sum(
        jnp.where(wide_code[:, :, :tok] == slot_f[None, :, :tok], wide_weight, 0.0),
        axis=2,
        keepdims=True,
    )

    own_code, _ = places(ids_t, combine_t, jnp.arange(experts, dtype=jnp.int32))
    depth = experts * columns * capacity
    back_to = iota((experts, depth), 1) // (columns * capacity)
    unfold = (iota((experts, depth), 0) == back_to).astype(BF16)
    wide_own = contract_rows(own_code.astype(BF16), unfold)
    at = iota((columns, tok, depth), 2)
    unpick = jnp.logical_and(
        wide_own[None] == (at % capacity).astype(F32),
        (at // capacity) % columns == iota((columns, tok, depth), 0),
    ).astype(BF16)

    send_rows = select_rows(pick, gathered, 0, half, n_y)
    send_grads = select_rows(pick, gathered, half, half, n_y, scale)
    rows_mine = lax.all_to_all(send_rows, "y", 0, 0, tiled=True)
    grads_mine = lax.all_to_all(send_grads, "y", 0, 0, tiled=True)
    rows_other = lax.ppermute(rows_mine, "section", swap)
    grads_other = lax.ppermute(grads_mine, "section", swap)

    shares = (n_tp, rows // n_tp, half)
    pre_part = pair_matmul(
        rows_mine.reshape(shares), rows_other.reshape(shares), both_mine, both_other
    )
    hidden_part = pair_matmul(
        grads_mine.reshape(shares), grads_other.reshape(shares), down_mine, down_other
    )
    pre_terms = lax.all_to_all(pre_part, "tp", 0, 0, tiled=True)
    hidden_terms = lax.all_to_all(hidden_part, "tp", 0, 0, tiled=True)
    pre = jnp.sum(pre_terms.astype(F32), axis=0)
    gate_pre, up_pre = pre[:, :hidden], pre[:, hidden:]
    hidden_grad = jnp.sum(hidden_terms.astype(F32), axis=0)
    sigmoid_g = jax.nn.sigmoid(gate_pre)
    activated = (gate_pre * sigmoid_g * up_pre).astype(BF16)
    gate_grad = hidden_grad * up_pre * sigmoid_g * (1.0 + gate_pre * (1.0 - sigmoid_g))
    up_grad = hidden_grad * gate_pre * sigmoid_g
    pre_grad = jnp.concatenate([gate_grad.astype(BF16), up_grad.astype(BF16)], axis=1)
    pre_grads = lax.all_to_all(
        jnp.broadcast_to(pre_grad[None], (n_tp,) + pre_grad.shape), "tp", 0, 0, tiled=True
    ).reshape(rows, 2 * hidden)
    activated_all = lax.all_gather(activated, "tp", axis=0, tiled=True)

    row_other = jnp.dot(pre_grads, back_other, preferred_element_type=F32).astype(BF16)
    row_got = lax.ppermute(row_other, "section", swap)
    row_mine = jnp.dot(pre_grads, back_mine, preferred_element_type=F32)
    packed = pack_rows(row_mine, row_got, capacity)
    returned = lax.all_to_all(
        packed.reshape(experts, columns * capacity, LANES), ("y", "z"), 0, 0, tiled=True
    )
    token_grad = combine_rows(unpick, returned.reshape(depth, LANES))

    first = section == 0
    rows_a, rows_b = rows_mine.reshape(rows, half), rows_other.reshape(rows, half)
    grads_a, grads_b = grads_mine.reshape(rows, half), grads_other.reshape(rows, half)
    both_a = contract_rows(rows_a, pre_grads).astype(BF16)
    both_b = contract_rows(rows_b, pre_grads).astype(BF16)
    down_a = contract_rows(activated_all, grads_a).astype(BF16)
    down_b = contract_rows(activated_all, grads_b).astype(BF16)
    both_wgrad = jnp.concatenate(
        [jnp.where(first, both_a, both_b), jnp.where(first, both_b, both_a)], axis=0
    )
    down_wgrad = jnp.concatenate(
        [jnp.where(first, down_a, down_b), jnp.where(first, down_b, down_a)], axis=1
    )
    return (
        token_grad,
        both_wgrad[None, :, :hidden],
        both_wgrad[None, :, hidden:],
        down_wgrad[None],
    )


def solution(mesh):
    n_y = 4
    shape = mesh.shape
    fine = Mesh(
        mesh.devices.reshape(shape["section"], n_y, shape["expert"] // n_y, shape["tp"]),
        ("section", "y", "z", "tp"),
    )
    expert = ("y", "z")
    return jax.shard_map(
        on_device,
        mesh=fine,
        in_specs=(
            P(expert, ("tp", "section")),
            P(expert, ("tp", "section")),
            P(expert, None),
            P(expert, None),
            P(expert, "tp", "section"),
            P(expert, "tp", "section"),
            P(expert, "section", "tp"),
        ),
        out_specs=(
            P(expert, ("tp", "section")),
            P(expert, "tp", "section"),
            P(expert, "tp", "section"),
            P(expert, "section", "tp"),
        ),
        check_vma=False,
    )
```

```python
import functools

import jax
import jax.numpy as jnp
import numpy as np
from jax import lax
from jax.experimental import pallas as pl
from jax.experimental.pallas import tpu as pltpu
from jax.sharding import Mesh
from jax.sharding import PartitionSpec as P

BF16 = jnp.bfloat16
F32 = jnp.float32
LANES = 128
SELECT_MIB = 56


def params(mib=20):
    return pltpu.CompilerParams(vmem_limit_bytes=mib << 20)


def iota(shape, dim):
    return lax.broadcasted_iota(jnp.int32, shape, dim)


def pick_groups(pick_ref, rows_ref, n_y, out_ref, scale_ref=None):
    groups, picked, span = pick_ref.shape
    part = picked // n_y
    pieces = []
    for g in range(groups):
        got = jnp.dot(
            pick_ref[g], rows_ref[g * span : (g + 1) * span, :], preferred_element_type=F32
        )
        pieces.append(got if scale_ref is None else got * scale_ref[g])
    for j in range(n_y):
        whole = jnp.concatenate([p[j * part : (j + 1) * part] for p in pieces], axis=0)
        out_ref[j] = whole.astype(BF16)


def select_tokens_kernel(n_y, place_ref, spread_ref, wanted_ref, *refs):
    blocks = refs[:-5]
    out_ref, pick_ref, scale_ref, notes, rows = refs[-5:]
    count = len(blocks)
    place = place_ref[0]
    tok = rows.shape[0] // count
    for i, block in enumerate(blocks):
        at = lax.rem(place + i, count)
        notes[at] = block[tok:, :].astype(F32)
        rows[pl.ds(pl.multiple_of(at * tok, tok), tok), :] = block[:tok, :]
    ids = notes[:, :, :tok]
    masks, weights = [], []
    for j in range(n_y):
        hit = ids == (j * count + place).astype(F32)
        masks.append(jnp.sum(jnp.where(hit, 1.0, 0.0), axis=1))
        weights.append(
            [
                jnp.sum(jnp.where(hit, notes[:, :, k * tok : (k + 1) * tok], 0.0), axis=1)
                for k in (1, 2, 3)
            ]
        )
    mask = jnp.concatenate(masks, axis=0)
    earlier = jnp.where(iota((tok, tok), 0) < iota((tok, tok), 1), 1.0, 0.0).astype(BF16)
    rank = jnp.dot(mask.astype(BF16), earlier, preferred_element_type=F32)
    code = jnp.where(mask > 0.5, rank, -1.0).astype(BF16)
    spread = spread_ref[...]
    wide = jnp.dot(spread, code, preferred_element_type=F32)
    weight = 0.0
    for k in (2, 1, 0):
        piece = jnp.concatenate([w[k] for w in weights], axis=0).astype(BF16)
        weight = weight + jnp.dot(spread, piece, preferred_element_type=F32)
    groups, picked, span = pick_ref.shape
    for g in range(groups):
        at = slice(g * picked, (g + 1) * picked)
        taken = jnp.zeros((picked, tok), F32)
        for z in range(span // tok):
            hit = jnp.where(wide[at] == wanted_ref[:, z : z + 1], 1.0, 0.0)
            pick_ref[g, :, z * tok : (z + 1) * tok] = hit.astype(BF16)
            taken = taken + hit
        scale_ref[g] = jnp.sum(taken * weight[at], axis=1, keepdims=True)
    pick_groups(pick_ref, rows, n_y, out_ref)


def select_tokens(blocks, place, spread, wanted, tok, n_y):
    count = len(blocks)
    group = wanted.shape[1]
    groups = count // group
    picked = wanted.shape[0]
    width = blocks[0].shape[1]
    extra = blocks[0].shape[0] - tok
    slots = groups * picked // n_y
    block = blocks[0].shape

    def whole(shape):
        return pl.BlockSpec(shape, lambda i: (0,) * len(shape))

    outs = [
        jax.ShapeDtypeStruct((n_y, slots, width), BF16),
        jax.ShapeDtypeStruct((groups, picked, group * tok), BF16),
        jax.ShapeDtypeStruct((groups, picked, 1), F32),
    ]
    return pl.pallas_call(
        functools.partial(select_tokens_kernel, n_y),
        grid=(1,),
        in_specs=[
            pl.BlockSpec(memory_space=pltpu.SMEM),
            whole(spread.shape),
            whole(wanted.shape),
        ]
        + [whole(block)] * count,
        out_specs=[whole(o.shape) for o in outs],
        out_shape=outs,
        scratch_shapes=[
            pltpu.VMEM((count, extra, width), F32),
            pltpu.VMEM((count * tok, width), BF16),
        ],
        compiler_params=params(SELECT_MIB),
        name="select_tokens",
    )(place, spread, wanted, *blocks)


def select_grads_kernel(n_y, pick_ref, rows_ref, scale_ref, out_ref):
    pick_groups(pick_ref, rows_ref, n_y, out_ref, scale_ref)


def select_grads(pick, rows, scale, n_y):
    groups, picked, span = pick.shape
    block = 256
    slots = groups * picked // n_y
    width = rows.shape[1]
    return pl.pallas_call(
        functools.partial(select_grads_kernel, n_y),
        grid=(width // block,),
        in_specs=[
            pl.BlockSpec((groups, picked, span), lambda i: (0, 0, 0)),
            pl.BlockSpec((groups * span, block), lambda i: (0, i)),
            pl.BlockSpec((groups, picked, 1), lambda i: (0, 0, 0)),
        ],
        out_specs=pl.BlockSpec((n_y, slots, block), lambda i: (0, 0, i)),
        out_shape=jax.ShapeDtypeStruct((n_y, slots, width), BF16),
        compiler_params=params(),
        name="select_grads",
    )(pick, rows, scale)


def pack_kernel(group, mine_ref, other_ref, order_ref, out_ref):
    rows = mine_ref.shape[0]
    columns = mine_ref.shape[1] // LANES
    total = mine_ref[...] + other_ref[...].astype(F32)
    for start in range(0, rows, group):
        piece = total[start : start + group]
        stacked = jnp.concatenate(
            [piece[:, q * LANES : (q + 1) * LANES] for q in range(columns)], axis=0
        )
        packed = jnp.dot(order_ref[...], stacked.astype(BF16), preferred_element_type=F32)
        out_ref[start * columns : (start + group) * columns, :] = packed.astype(BF16)


def pack_order(columns, capacity, blocks):
    size = blocks * columns * capacity
    at = np.arange(size)
    b, q, c = at // (columns * capacity), (at // capacity) % columns, at % capacity
    order = np.zeros((size, size), np.float32)
    order[at, q * blocks * capacity + b * capacity + c] = 1.0
    return order


def pack_rows(mine, other, capacity):
    rows, width = mine.shape
    columns = width // LANES
    group = 4 * capacity
    size = group * columns
    order = jnp.asarray(pack_order(columns, capacity, 4), BF16)
    steps = 4
    return pl.pallas_call(
        functools.partial(pack_kernel, group),
        grid=(steps,),
        in_specs=[
            pl.BlockSpec((rows // steps, width), lambda i: (i, 0)),
            pl.BlockSpec((rows // steps, width), lambda i: (i, 0)),
            pl.BlockSpec((size, size), lambda i: (0, 0)),
        ],
        out_specs=pl.BlockSpec((rows * columns // steps, LANES), lambda i: (i, 0)),
        out_shape=jax.ShapeDtypeStruct((rows * columns, LANES), BF16),
        compiler_params=params(),
        name="pack_rows",
    )(mine, other, order)


def combine_kernel(group, pick_ref, order_ref, rows_ref, out_ref, flat):
    rows, width = flat.shape
    columns = width // LANES
    size = group * columns
    for start in range(0, rows, 2 * group):
        at = start * columns
        two = jnp.concatenate(
            [rows_ref[at : at + size, :], rows_ref[at + size : at + 2 * size, :]], axis=1
        )
        plain = jnp.dot(order_ref[...], two, preferred_element_type=F32)
        for q in range(columns):
            part = plain[q * group : (q + 1) * group]
            lanes = slice(q * LANES, (q + 1) * LANES)
            flat[start : start + group, lanes] = part[:, :LANES]
            flat[start + group : start + 2 * group, lanes] = part[:, LANES:]
    total = jnp.dot(pick_ref[...], flat[...].astype(BF16), preferred_element_type=F32)
    out_ref[...] = total.astype(BF16)


def combine_rows(pick, rows, capacity):
    tok, slots = pick.shape
    columns = rows.shape[0] // slots
    width = columns * LANES
    order = jnp.asarray(pack_order(columns, capacity, 4).T, BF16)
    return pl.pallas_call(
        functools.partial(combine_kernel, 4 * capacity),
        out_shape=jax.ShapeDtypeStruct((tok, width), BF16),
        scratch_shapes=[pltpu.VMEM((slots, width), F32)],
        compiler_params=params(),
        name="combine_rows",
    )(pick, order, rows)


def own_places(ids_t, experts):
    tok = ids_t.shape[1]
    names = jnp.arange(experts, dtype=jnp.int32)
    mask = jnp.any(ids_t[None, :, :] == names[:, None, None], axis=1)
    earlier = (iota((tok, tok), 0) < iota((tok, tok), 1)).astype(BF16)
    rank = jnp.dot(mask.astype(BF16), earlier, preferred_element_type=F32)
    return jnp.where(mask, rank, -1.0)


def three_parts(values):
    parts = []
    for _ in range(3):
        part = lax.reduce_precision(values, 8, 7)
        parts.append(part.astype(BF16))
        values = values - part
    return parts


def dot(left, right):
    return jnp.dot(left, right, preferred_element_type=F32)


def contract_rows(left, right):
    return lax.dot_general(left, right, (((0,), (0,)), ((), ())), preferred_element_type=F32)


def on_device(tokens, out_grad, expert_ids, combine, w_gate, w_up, w_down):
    tok, top = expert_ids.shape
    n_y, n_z = lax.axis_size("y"), lax.axis_size("z")
    n_tp = lax.axis_size("tp")
    experts = n_y * n_z
    capacity = (tok * top * 9 + 8 * experts - 1) // (8 * experts)
    half = tokens.shape[1]
    columns = half // LANES
    group = 4
    groups = n_z // group
    rows = experts * capacity
    section = lax.axis_index("section")
    swap = [(0, 1), (1, 0)]

    grads_all = lax.all_gather(out_grad, "z", axis=0, tiled=True)

    both = jnp.concatenate([w_gate[0], w_up[0]], axis=1)
    hidden = w_gate.shape[2]
    down_t = w_down[0].T
    both_mine = lax.dynamic_slice_in_dim(both, section * half, half, 0)
    both_other = lax.dynamic_slice_in_dim(both, (1 - section) * half, half, 0)
    down_mine = lax.dynamic_slice_in_dim(down_t, section * half, half, 0)
    down_other = lax.dynamic_slice_in_dim(down_t, (1 - section) * half, half, 0)
    back_mine, back_other = both_mine.T, both_other.T

    ids_t, combine_t = expert_ids.T, combine.T
    notes = jnp.concatenate([ids_t.astype(BF16)] + three_parts(combine_t), axis=1)

    ahead = [(i, (i + 1) % n_z) for i in range(n_z)]
    back = [(i, (i - 1) % n_z) for i in range(n_z)]
    ring = [None] * n_z
    ring[0] = low = high = jnp.concatenate([tokens, notes], axis=0)
    for step in range(1, n_z // 2 + 1):
        low = lax.ppermute(low, "z", ahead)
        ring[n_z - step] = low
        if step < n_z // 2:
            high = lax.ppermute(high, "z", back)
            ring[step] = high

    spot = np.arange(rows)
    sub = (spot // capacity) % group
    of_y = (spot // (group * capacity)) % n_y
    source = of_y * n_z + spot // (n_y * group * capacity) * group + sub
    spread = (source[:, None] == np.arange(experts)[None, :]).astype(np.float32)
    spot = spot[: rows // groups]
    same = ((spot // capacity) % group)[:, None] == np.arange(group)[None, :]
    wanted = np.where(same, (spot % capacity)[:, None], -7).astype(np.float32)
    place = lax.axis_index("z").reshape(1)
    own_code = own_places(ids_t, experts)
    slots = np.arange(rows)
    unfold = (np.arange(experts)[:, None] == (slots // capacity)[None, :]).astype(np.float32)
    wide_own = contract_rows(own_code.astype(BF16), jnp.asarray(unfold, BF16))
    own_slot = jnp.asarray((slots % capacity).astype(np.float32))[None, :]
    unpick = (wide_own == own_slot).astype(BF16)

    send_rows, pick, scale = select_tokens(
        ring, place, jnp.asarray(spread, BF16), jnp.asarray(wanted), tok, n_y
    )
    send_rows, grads_all = lax.optimization_barrier((send_rows, grads_all))
    rows_mine = lax.all_to_all(send_rows, "y", 0, 0, tiled=True).reshape(rows, half)
    send_grads = select_grads(pick, grads_all, scale, n_y)
    rows_mine, send_grads = lax.optimization_barrier((rows_mine, send_grads))
    rows_other = lax.ppermute(rows_mine, "section", swap)
    grads_mine = lax.all_to_all(send_grads, "y", 0, 0, tiled=True).reshape(rows, half)
    grads_other = lax.ppermute(grads_mine, "section", swap)

    pre_part = (dot(rows_mine, both_mine) + dot(rows_other, both_other)).astype(BF16)
    hidden_part = (dot(grads_mine, down_mine) + dot(grads_other, down_other)).astype(BF16)
    pre = lax.psum_scatter(pre_part, "tp", scatter_dimension=0, tiled=True)
    hidden_terms = lax.all_to_all(
        hidden_part.reshape(n_tp, rows // n_tp, hidden), "tp", 0, 0, tiled=True
    )
    gate_pre, up_pre = pre[:, :hidden].astype(F32), pre[:, hidden:].astype(F32)
    hidden_grad = jnp.sum(hidden_terms.astype(F32), axis=0)
    sigmoid_g = jax.nn.sigmoid(gate_pre)
    activated = (gate_pre * sigmoid_g * up_pre).astype(BF16)
    gate_grad = hidden_grad * up_pre * sigmoid_g * (1.0 + gate_pre * (1.0 - sigmoid_g))
    up_grad = hidden_grad * gate_pre * sigmoid_g
    pre_grad = jnp.concatenate([gate_grad.astype(BF16), up_grad.astype(BF16)], axis=1)
    pre_grads = lax.all_to_all(
        jnp.broadcast_to(pre_grad[None], (n_tp,) + pre_grad.shape), "tp", 0, 0, tiled=True
    ).reshape(rows, 2 * hidden)
    activated_all = lax.all_gather(activated, "tp", axis=0, tiled=True)

    row_other = dot(pre_grads, back_other).astype(BF16)
    row_got = lax.ppermute(row_other, "section", swap)
    row_mine = dot(pre_grads, back_mine)
    packed = pack_rows(row_mine, row_got, capacity)
    returned = lax.all_to_all(
        packed.reshape(experts, columns * capacity, LANES), ("y", "z"), 0, 0, tiled=True
    )
    token_grad = combine_rows(unpick, returned.reshape(rows * columns, LANES), capacity)

    first = section == 0
    both_a = contract_rows(rows_mine, pre_grads).astype(BF16)
    both_b = contract_rows(rows_other, pre_grads).astype(BF16)
    down_a = contract_rows(activated_all, grads_mine).astype(BF16)
    down_b = contract_rows(activated_all, grads_other).astype(BF16)
    both_wgrad = jnp.concatenate(
        [jnp.where(first, both_a, both_b), jnp.where(first, both_b, both_a)], axis=0
    )
    down_wgrad = jnp.concatenate(
        [jnp.where(first, down_a, down_b), jnp.where(first, down_b, down_a)], axis=1
    )
    return (
        token_grad,
        both_wgrad[None, :, :hidden],
        both_wgrad[None, :, hidden:],
        down_wgrad[None],
    )


def solution(mesh):
    n_y = 4
    shape = mesh.shape
    fine = Mesh(
        mesh.devices.reshape(shape["section"], n_y, shape["expert"] // n_y, shape["tp"]),
        ("section", "y", "z", "tp"),
    )
    expert = ("y", "z")
    return jax.shard_map(
        on_device,
        mesh=fine,
        in_specs=(
            P(expert, ("tp", "section")),
            P(expert, ("tp", "section")),
            P(expert, None),
            P(expert, None),
            P(expert, "tp", "section"),
            P(expert, "tp", "section"),
            P(expert, "section", "tp"),
        ),
        out_specs=(
            P(expert, ("tp", "section")),
            P(expert, "tp", "section"),
            P(expert, "tp", "section"),
            P(expert, "section", "tp"),
        ),
        check_vma=False,
    )
```

```python
import functools

import jax
import jax.numpy as jnp
import numpy as np
from jax import lax
from jax.experimental import pallas as pl
from jax.experimental.pallas import tpu as pltpu
from jax.sharding import Mesh
from jax.sharding import PartitionSpec as P

BF16 = jnp.bfloat16
F32 = jnp.float32
LANES = 128
SELECT_MIB = 56


def params(mib=20):
    return pltpu.CompilerParams(vmem_limit_bytes=mib << 20)


def iota(shape, dim):
    return lax.broadcasted_iota(jnp.int32, shape, dim)


def pick_groups(pick_ref, rows_ref, n_y, out_ref, scale_ref=None):
    groups, picked, span = pick_ref.shape
    part = picked // n_y
    pieces = []
    for g in range(groups):
        got = jnp.dot(
            pick_ref[g], rows_ref[g * span : (g + 1) * span, :], preferred_element_type=F32
        )
        pieces.append(got if scale_ref is None else got * scale_ref[g])
    for j in range(n_y):
        whole = jnp.concatenate([p[j * part : (j + 1) * part] for p in pieces], axis=0)
        out_ref[j] = whole.astype(BF16)


def select_tokens_kernel(n_y, place_ref, spread_ref, wanted_ref, *refs):
    blocks = refs[:-5]
    out_ref, pick_ref, scale_ref, notes, rows = refs[-5:]
    count = len(blocks)
    place = place_ref[0]
    tok = rows.shape[0] // count
    for i, block in enumerate(blocks):
        at = lax.rem(place + i * place_ref[1], count)
        notes[at] = block[tok:, :].astype(F32)
        rows[pl.ds(pl.multiple_of(at * tok, tok), tok), :] = block[:tok, :]
    ids = notes[:, :, :tok]
    masks, weights = [], []
    for j in range(n_y):
        hit = ids == (j * count + place).astype(F32)
        masks.append(jnp.sum(jnp.where(hit, 1.0, 0.0), axis=1))
        weights.append(
            [
                jnp.sum(jnp.where(hit, notes[:, :, k * tok : (k + 1) * tok], 0.0), axis=1)
                for k in (1, 2, 3)
            ]
        )
    mask = jnp.concatenate(masks, axis=0)
    earlier = jnp.where(iota((tok, tok), 0) < iota((tok, tok), 1), 1.0, 0.0).astype(BF16)
    rank = jnp.dot(mask.astype(BF16), earlier, preferred_element_type=F32)
    code = jnp.where(mask > 0.5, rank, -1.0).astype(BF16)
    spread = spread_ref[...]
    wide = jnp.dot(spread, code, preferred_element_type=F32)
    weight = 0.0
    for k in (2, 1, 0):
        piece = jnp.concatenate([w[k] for w in weights], axis=0).astype(BF16)
        weight = weight + jnp.dot(spread, piece, preferred_element_type=F32)
    groups, picked, span = pick_ref.shape
    for g in range(groups):
        at = slice(g * picked, (g + 1) * picked)
        taken = jnp.zeros((picked, tok), F32)
        for z in range(span // tok):
            hit = jnp.where(wide[at] == wanted_ref[:, z : z + 1], 1.0, 0.0)
            pick_ref[g, :, z * tok : (z + 1) * tok] = hit.astype(BF16)
            taken = taken + hit
        scale_ref[g] = jnp.sum(taken * weight[at], axis=1, keepdims=True)
    pick_groups(pick_ref, rows, n_y, out_ref)


def select_tokens(blocks, place, spread, wanted, tok, n_y):
    count = len(blocks)
    group = wanted.shape[1]
    groups = count // group
    picked = wanted.shape[0]
    width = blocks[0].shape[1]
    extra = blocks[0].shape[0] - tok
    slots = groups * picked // n_y
    block = blocks[0].shape

    def whole(shape):
        return pl.BlockSpec(shape, lambda i: (0,) * len(shape))

    outs = [
        jax.ShapeDtypeStruct((n_y, slots, width), BF16),
        jax.ShapeDtypeStruct((groups, picked, group * tok), BF16),
        jax.ShapeDtypeStruct((groups, picked, 1), F32),
    ]
    return pl.pallas_call(
        functools.partial(select_tokens_kernel, n_y),
        grid=(1,),
        in_specs=[
            pl.BlockSpec(memory_space=pltpu.SMEM),
            whole(spread.shape),
            whole(wanted.shape),
        ]
        + [whole(block)] * count,
        out_specs=[whole(o.shape) for o in outs],
        out_shape=outs,
        scratch_shapes=[
            pltpu.VMEM((count, extra, width), F32),
            pltpu.VMEM((count * tok, width), BF16),
        ],
        compiler_params=params(SELECT_MIB),
        name="select_tokens",
    )(place, spread, wanted, *blocks)


def select_grads_kernel(n_y, pick_ref, rows_ref, scale_ref, out_ref):
    pick_groups(pick_ref, rows_ref, n_y, out_ref, scale_ref)


def select_grads(pick, rows, scale, n_y):
    groups, picked, span = pick.shape
    block = 256
    slots = groups * picked // n_y
    width = rows.shape[1]
    return pl.pallas_call(
        functools.partial(select_grads_kernel, n_y),
        grid=(width // block,),
        in_specs=[
            pl.BlockSpec((groups, picked, span), lambda i: (0, 0, 0)),
            pl.BlockSpec((groups * span, block), lambda i: (0, i)),
            pl.BlockSpec((groups, picked, 1), lambda i: (0, 0, 0)),
        ],
        out_specs=pl.BlockSpec((n_y, slots, block), lambda i: (0, 0, i)),
        out_shape=jax.ShapeDtypeStruct((n_y, slots, width), BF16),
        compiler_params=params(),
        name="select_grads",
    )(pick, rows, scale)


def pack_kernel(group, mine_ref, other_ref, order_ref, out_ref):
    rows = mine_ref.shape[0]
    columns = mine_ref.shape[1] // LANES
    total = mine_ref[...] + other_ref[...].astype(F32)
    for start in range(0, rows, group):
        piece = total[start : start + group]
        stacked = jnp.concatenate(
            [piece[:, q * LANES : (q + 1) * LANES] for q in range(columns)], axis=0
        )
        packed = jnp.dot(order_ref[...], stacked.astype(BF16), preferred_element_type=F32)
        out_ref[start * columns : (start + group) * columns, :] = packed.astype(BF16)


def pack_order(columns, capacity, blocks):
    size = blocks * columns * capacity
    at = np.arange(size)
    b, q, c = at // (columns * capacity), (at // capacity) % columns, at % capacity
    order = np.zeros((size, size), np.float32)
    order[at, q * blocks * capacity + b * capacity + c] = 1.0
    return order


def pack_rows(mine, other, capacity):
    rows, width = mine.shape
    columns = width // LANES
    group = 4 * capacity
    size = group * columns
    order = jnp.asarray(pack_order(columns, capacity, 4), BF16)
    steps = 4
    return pl.pallas_call(
        functools.partial(pack_kernel, group),
        grid=(steps,),
        in_specs=[
            pl.BlockSpec((rows // steps, width), lambda i: (i, 0)),
            pl.BlockSpec((rows // steps, width), lambda i: (i, 0)),
            pl.BlockSpec((size, size), lambda i: (0, 0)),
        ],
        out_specs=pl.BlockSpec((rows * columns // steps, LANES), lambda i: (i, 0)),
        out_shape=jax.ShapeDtypeStruct((rows * columns, LANES), BF16),
        compiler_params=params(),
        name="pack_rows",
    )(mine, other, order)


def combine_kernel(group, pick_ref, order_ref, rows_ref, out_ref, flat):
    rows, width = flat.shape
    columns = width // LANES
    size = group * columns
    for start in range(0, rows, 2 * group):
        at = start * columns
        two = jnp.concatenate(
            [rows_ref[at : at + size, :], rows_ref[at + size : at + 2 * size, :]], axis=1
        )
        plain = jnp.dot(order_ref[...], two, preferred_element_type=F32)
        for q in range(columns):
            part = plain[q * group : (q + 1) * group]
            lanes = slice(q * LANES, (q + 1) * LANES)
            flat[start : start + group, lanes] = part[:, :LANES]
            flat[start + group : start + 2 * group, lanes] = part[:, LANES:]
    total = jnp.dot(pick_ref[...], flat[...].astype(BF16), preferred_element_type=F32)
    out_ref[...] = total.astype(BF16)


def combine_rows(pick, rows, capacity):
    tok, slots = pick.shape
    columns = rows.shape[0] // slots
    width = columns * LANES
    order = jnp.asarray(pack_order(columns, capacity, 4).T, BF16)
    return pl.pallas_call(
        functools.partial(combine_kernel, 4 * capacity),
        out_shape=jax.ShapeDtypeStruct((tok, width), BF16),
        scratch_shapes=[pltpu.VMEM((slots, width), F32)],
        compiler_params=params(),
        name="combine_rows",
    )(pick, order, rows)


def own_places(ids_t, experts):
    tok = ids_t.shape[1]
    names = jnp.arange(experts, dtype=jnp.int32)
    mask = jnp.any(ids_t[None, :, :] == names[:, None, None], axis=1)
    earlier = (iota((tok, tok), 0) < iota((tok, tok), 1)).astype(BF16)
    rank = jnp.dot(mask.astype(BF16), earlier, preferred_element_type=F32)
    return jnp.where(mask, rank, -1.0)


def block_kernel(tokens_ref, ids_ref, combine_ref, out_ref):
    tok = tokens_ref.shape[0]
    out_ref[:tok, :] = tokens_ref[...]
    parts = [ids_ref[...].astype(F32).astype(BF16)]
    left = combine_ref[...]
    for _ in range(3):
        part = left.astype(BF16)
        parts.append(part)
        left = left - part.astype(F32)
    out_ref[tok:, :] = jnp.concatenate(parts, axis=1)


def first_block(tokens, ids_t, combine_t):
    tok, width = tokens.shape
    return pl.pallas_call(
        block_kernel,
        out_shape=jax.ShapeDtypeStruct((tok + ids_t.shape[0], width), BF16),
        compiler_params=params(),
        name="first_block",
    )(tokens, ids_t, combine_t)


def dot(left, right):
    return jnp.dot(left, right, preferred_element_type=F32)


def contract_rows(left, right):
    return lax.dot_general(left, right, (((0,), (0,)), ((), ())), preferred_element_type=F32)


def on_device(tokens, out_grad, expert_ids, combine, w_gate, w_up, w_down):
    tok, top = expert_ids.shape
    n_y, n_z = lax.axis_size("y"), lax.axis_size("z")
    n_tp = lax.axis_size("tp")
    experts = n_y * n_z
    capacity = (tok * top * 9 + 8 * experts - 1) // (8 * experts)
    half = tokens.shape[1]
    columns = half // LANES
    group = 4
    groups = n_z // group
    rows = experts * capacity
    section = lax.axis_index("section")
    swap = [(0, 1), (1, 0)]

    grads_all = lax.all_gather(out_grad, "z", axis=0, tiled=True)

    both = jnp.concatenate([w_gate[0], w_up[0]], axis=1)
    hidden = w_gate.shape[2]
    down_t = w_down[0].T
    both_mine = lax.dynamic_slice_in_dim(both, section * half, half, 0)
    both_other = lax.dynamic_slice_in_dim(both, (1 - section) * half, half, 0)
    down_mine = lax.dynamic_slice_in_dim(down_t, section * half, half, 0)
    down_other = lax.dynamic_slice_in_dim(down_t, (1 - section) * half, half, 0)
    back_mine, back_other = both_mine.T, both_other.T

    ids_t, combine_t = expert_ids.T, combine.T

    ahead = [(c * n_z + i, c * n_z + (i + 1 - 2 * c) % n_z) for c in (0, 1) for i in range(n_z)]
    back = [(to, frm) for frm, to in ahead]
    ring = [None] * n_z
    ring[0] = low = high = first_block(tokens, ids_t, combine_t)
    for step in range(1, n_z // 2 + 1):
        low = lax.ppermute(low, ("section", "z"), ahead)
        ring[n_z - step] = low
        if step < n_z // 2:
            high = lax.ppermute(high, ("section", "z"), back)
            ring[step] = high

    spot = np.arange(rows)
    sub = (spot // capacity) % group
    of_y = (spot // (group * capacity)) % n_y
    source = of_y * n_z + spot // (n_y * group * capacity) * group + sub
    spread = (source[:, None] == np.arange(experts)[None, :]).astype(np.float32)
    spot = spot[: rows // groups]
    same = ((spot // capacity) % group)[:, None] == np.arange(group)[None, :]
    wanted = np.where(same, (spot % capacity)[:, None], -7).astype(np.float32)
    place = jnp.stack([lax.axis_index("z"), jnp.where(section == 0, 1, n_z - 1)])
    own_code = own_places(ids_t, experts)
    slots = np.arange(rows)
    unfold = (np.arange(experts)[:, None] == (slots // capacity)[None, :]).astype(np.float32)
    wide_own = contract_rows(own_code.astype(BF16), jnp.asarray(unfold, BF16))
    own_slot = jnp.asarray((slots % capacity).astype(np.float32))[None, :]
    unpick = (wide_own == own_slot).astype(BF16)

    send_rows, pick, scale = select_tokens(
        ring, place, jnp.asarray(spread, BF16), jnp.asarray(wanted), tok, n_y
    )
    send_rows, grads_all = lax.optimization_barrier((send_rows, grads_all))
    rows_mine = lax.all_to_all(send_rows, "y", 0, 0, tiled=True).reshape(rows, half)
    send_grads = select_grads(pick, grads_all, scale, n_y)
    rows_mine, send_grads = lax.optimization_barrier((rows_mine, send_grads))
    rows_other = lax.ppermute(rows_mine, "section", swap)
    grads_mine = lax.all_to_all(send_grads, "y", 0, 0, tiled=True).reshape(rows, half)
    grads_other = lax.ppermute(grads_mine, "section", swap)

    pre_part = (dot(rows_mine, both_mine) + dot(rows_other, both_other)).astype(BF16)
    hidden_part = (dot(grads_mine, down_mine) + dot(grads_other, down_other)).astype(BF16)
    pre = lax.psum_scatter(pre_part, "tp", scatter_dimension=0, tiled=True)
    hidden_terms = lax.all_to_all(
        hidden_part.reshape(n_tp, rows // n_tp, hidden), "tp", 0, 0, tiled=True
    )
    gate_pre, up_pre = pre[:, :hidden].astype(F32), pre[:, hidden:].astype(F32)
    hidden_grad = jnp.sum(hidden_terms.astype(F32), axis=0)
    sigmoid_g = jax.nn.sigmoid(gate_pre)
    activated = (gate_pre * sigmoid_g * up_pre).astype(BF16)
    gate_grad = hidden_grad * up_pre * sigmoid_g * (1.0 + gate_pre * (1.0 - sigmoid_g))
    up_grad = hidden_grad * gate_pre * sigmoid_g
    pre_grad = jnp.concatenate([gate_grad.astype(BF16), up_grad.astype(BF16)], axis=1)
    pre_grads = lax.all_to_all(
        jnp.broadcast_to(pre_grad[None], (n_tp,) + pre_grad.shape), "tp", 0, 0, tiled=True
    ).reshape(rows, 2 * hidden)
    activated_all = lax.all_gather(activated, "tp", axis=0, tiled=True)

    row_other = dot(pre_grads, back_other).astype(BF16)
    row_got = lax.ppermute(row_other, "section", swap)
    row_mine = dot(pre_grads, back_mine)
    packed = pack_rows(row_mine, row_got, capacity)
    returned = lax.all_to_all(
        packed.reshape(experts, columns * capacity, LANES), ("y", "z"), 0, 0, tiled=True
    )
    token_grad = combine_rows(unpick, returned.reshape(rows * columns, LANES), capacity)

    first = section == 0
    both_a = contract_rows(rows_mine, pre_grads).astype(BF16)
    both_b = contract_rows(rows_other, pre_grads).astype(BF16)
    down_a = contract_rows(activated_all, grads_mine).astype(BF16)
    down_b = contract_rows(activated_all, grads_other).astype(BF16)
    both_wgrad = jnp.concatenate(
        [jnp.where(first, both_a, both_b), jnp.where(first, both_b, both_a)], axis=0
    )
    down_wgrad = jnp.concatenate(
        [jnp.where(first, down_a, down_b), jnp.where(first, down_b, down_a)], axis=1
    )
    return (
        token_grad,
        both_wgrad[None, :, :hidden],
        both_wgrad[None, :, hidden:],
        down_wgrad[None],
    )


def solution(mesh):
    n_y = 4
    shape = mesh.shape
    fine = Mesh(
        mesh.devices.reshape(shape["section"], n_y, shape["expert"] // n_y, shape["tp"]),
        ("section", "y", "z", "tp"),
    )
    expert = ("y", "z")
    return jax.shard_map(
        on_device,
        mesh=fine,
        in_specs=(
            P(expert, ("tp", "section")),
            P(expert, ("tp", "section")),
            P(expert, None),
            P(expert, None),
            P(expert, "tp", "section"),
            P(expert, "tp", "section"),
            P(expert, "section", "tp"),
        ),
        out_specs=(
            P(expert, ("tp", "section")),
            P(expert, "tp", "section"),
            P(expert, "tp", "section"),
            P(expert, "section", "tp"),
        ),
        check_vma=False,
    )
```

```python
import functools

import jax
import jax.numpy as jnp
import numpy as np
from jax import lax
from jax.experimental import pallas as pl
from jax.experimental.pallas import tpu as pltpu
from jax.sharding import Mesh
from jax.sharding import PartitionSpec as P

BF16 = jnp.bfloat16
F32 = jnp.float32
LANES = 128
SELECT_MIB = 56


def params(mib=20):
    return pltpu.CompilerParams(vmem_limit_bytes=mib << 20)


def iota(shape, dim):
    return lax.broadcasted_iota(jnp.int32, shape, dim)


def pick_groups(pick_ref, rows_ref, n_y, out_ref, scale_ref=None):
    groups, picked, span = pick_ref.shape
    part = picked // n_y
    pieces = []
    for g in range(groups):
        got = jnp.dot(
            pick_ref[g], rows_ref[g * span : (g + 1) * span, :], preferred_element_type=F32
        )
        pieces.append(got if scale_ref is None else got * scale_ref[g])
    for j in range(n_y):
        whole = jnp.concatenate([p[j * part : (j + 1) * part] for p in pieces], axis=0)
        out_ref[j] = whole.astype(BF16)


def select_tokens_kernel(n_y, place_ref, spread_ref, wanted_ref, *refs):
    blocks = refs[:-5]
    out_ref, pick_ref, scale_ref, notes, rows = refs[-5:]
    count = len(blocks)
    place = place_ref[0]
    tok = rows.shape[0] // count
    for i, block in enumerate(blocks):
        at = lax.rem(place + i * place_ref[1], count)
        notes[at] = block[tok:, :].astype(F32)
        rows[pl.ds(pl.multiple_of(at * tok, tok), tok), :] = block[:tok, :]
    ids = notes[:, :, :tok]
    masks, weights = [], []
    for j in range(n_y):
        hit = ids == (j * count + place).astype(F32)
        masks.append(jnp.sum(jnp.where(hit, 1.0, 0.0), axis=1))
        weights.append(
            [
                jnp.sum(jnp.where(hit, notes[:, :, k * tok : (k + 1) * tok], 0.0), axis=1)
                for k in (1, 2, 3)
            ]
        )
    mask = jnp.concatenate(masks, axis=0)
    earlier = jnp.where(iota((tok, tok), 0) < iota((tok, tok), 1), 1.0, 0.0).astype(BF16)
    rank = jnp.dot(mask.astype(BF16), earlier, preferred_element_type=F32)
    code = jnp.where(mask > 0.5, rank, -1.0).astype(BF16)
    spread = spread_ref[...]
    wide = jnp.dot(spread, code, preferred_element_type=F32)
    weight = 0.0
    for k in (2, 1, 0):
        piece = jnp.concatenate([w[k] for w in weights], axis=0).astype(BF16)
        weight = weight + jnp.dot(spread, piece, preferred_element_type=F32)
    groups, picked, span = pick_ref.shape
    for g in range(groups):
        at = slice(g * picked, (g + 1) * picked)
        taken = jnp.zeros((picked, tok), F32)
        for z in range(span // tok):
            hit = jnp.where(wide[at] == wanted_ref[:, z : z + 1], 1.0, 0.0)
            pick_ref[g, :, z * tok : (z + 1) * tok] = hit.astype(BF16)
            taken = taken + hit
        scale_ref[g] = jnp.sum(taken * weight[at], axis=1, keepdims=True)
    pick_groups(pick_ref, rows, n_y, out_ref)


def select_tokens(blocks, place, spread, wanted, tok, n_y):
    count = len(blocks)
    group = wanted.shape[1]
    groups = count // group
    picked = wanted.shape[0]
    width = blocks[0].shape[1]
    extra = blocks[0].shape[0] - tok
    slots = groups * picked // n_y
    block = blocks[0].shape

    def whole(shape):
        return pl.BlockSpec(shape, lambda i: (0,) * len(shape))

    outs = [
        jax.ShapeDtypeStruct((n_y, slots, width), BF16),
        jax.ShapeDtypeStruct((groups, picked, group * tok), BF16),
        jax.ShapeDtypeStruct((groups, picked, 1), F32),
    ]
    return pl.pallas_call(
        functools.partial(select_tokens_kernel, n_y),
        grid=(1,),
        in_specs=[
            pl.BlockSpec(memory_space=pltpu.SMEM),
            whole(spread.shape),
            whole(wanted.shape),
        ]
        + [whole(block)] * count,
        out_specs=[whole(o.shape) for o in outs],
        out_shape=outs,
        scratch_shapes=[
            pltpu.VMEM((count, extra, width), F32),
            pltpu.VMEM((count * tok, width), BF16),
        ],
        compiler_params=params(SELECT_MIB),
        name="select_tokens",
    )(place, spread, wanted, *blocks)


def select_grads_kernel(n_y, pick_ref, rows_ref, scale_ref, out_ref):
    pick_groups(pick_ref, rows_ref, n_y, out_ref, scale_ref)


def select_grads(pick, rows, scale, n_y):
    groups, picked, span = pick.shape
    block = 256
    slots = groups * picked // n_y
    width = rows.shape[1]
    return pl.pallas_call(
        functools.partial(select_grads_kernel, n_y),
        grid=(width // block,),
        in_specs=[
            pl.BlockSpec((groups, picked, span), lambda i: (0, 0, 0)),
            pl.BlockSpec((groups * span, block), lambda i: (0, i)),
            pl.BlockSpec((groups, picked, 1), lambda i: (0, 0, 0)),
        ],
        out_specs=pl.BlockSpec((n_y, slots, block), lambda i: (0, 0, i)),
        out_shape=jax.ShapeDtypeStruct((n_y, slots, width), BF16),
        compiler_params=params(),
        name="select_grads",
    )(pick, rows, scale)


def pack_kernel(group, mine_ref, other_ref, order_ref, out_ref):
    rows = mine_ref.shape[0]
    columns = mine_ref.shape[1] // LANES
    total = mine_ref[...] + other_ref[...].astype(F32)
    size = group * columns
    for start in range(0, rows, 2 * group):
        pair = [
            jnp.concatenate(
                [total[at : at + group, q * LANES : (q + 1) * LANES] for q in range(columns)],
                axis=0,
            )
            for at in (start, start + group)
        ]
        stacked = jnp.concatenate(pair, axis=1).astype(BF16)
        packed = jnp.dot(order_ref[...], stacked, preferred_element_type=F32).astype(BF16)
        at = start * columns
        out_ref[at : at + size, :] = packed[:, :LANES]
        out_ref[at + size : at + 2 * size, :] = packed[:, LANES:]


def pack_order(columns, capacity, blocks):
    size = blocks * columns * capacity
    at = np.arange(size)
    b, q, c = at // (columns * capacity), (at // capacity) % columns, at % capacity
    order = np.zeros((size, size), np.float32)
    order[at, q * blocks * capacity + b * capacity + c] = 1.0
    return order


def pack_rows(mine, other, capacity):
    rows, width = mine.shape
    columns = width // LANES
    group = 4 * capacity
    size = group * columns
    order = jnp.asarray(pack_order(columns, capacity, 4), BF16)
    steps = 4
    return pl.pallas_call(
        functools.partial(pack_kernel, group),
        grid=(steps,),
        in_specs=[
            pl.BlockSpec((rows // steps, width), lambda i: (i, 0)),
            pl.BlockSpec((rows // steps, width), lambda i: (i, 0)),
            pl.BlockSpec((size, size), lambda i: (0, 0)),
        ],
        out_specs=pl.BlockSpec((rows * columns // steps, LANES), lambda i: (i, 0)),
        out_shape=jax.ShapeDtypeStruct((rows * columns, LANES), BF16),
        compiler_params=params(),
        name="pack_rows",
    )(mine, other, order)


def combine_kernel(group, pick_ref, order_ref, rows_ref, out_ref, flat):
    rows, width = flat.shape
    columns = width // LANES
    size = group * columns
    for start in range(0, rows, 2 * group):
        at = start * columns
        two = jnp.concatenate(
            [rows_ref[at : at + size, :], rows_ref[at + size : at + 2 * size, :]], axis=1
        )
        plain = jnp.dot(order_ref[...], two, preferred_element_type=F32)
        for q in range(columns):
            part = plain[q * group : (q + 1) * group]
            lanes = slice(q * LANES, (q + 1) * LANES)
            flat[start : start + group, lanes] = part[:, :LANES]
            flat[start + group : start + 2 * group, lanes] = part[:, LANES:]
    total = jnp.dot(pick_ref[...], flat[...].astype(BF16), preferred_element_type=F32)
    out_ref[...] = total.astype(BF16)


def combine_rows(pick, rows, capacity):
    tok, slots = pick.shape
    columns = rows.shape[0] // slots
    width = columns * LANES
    order = jnp.asarray(pack_order(columns, capacity, 4).T, BF16)
    return pl.pallas_call(
        functools.partial(combine_kernel, 4 * capacity),
        out_shape=jax.ShapeDtypeStruct((tok, width), BF16),
        scratch_shapes=[pltpu.VMEM((slots, width), F32)],
        compiler_params=params(),
        name="combine_rows",
    )(pick, order, rows)


def own_places(ids_t, experts):
    tok = ids_t.shape[1]
    names = jnp.arange(experts, dtype=jnp.int32)
    mask = jnp.any(ids_t[None, :, :] == names[:, None, None], axis=1)
    earlier = (iota((tok, tok), 0) < iota((tok, tok), 1)).astype(BF16)
    rank = jnp.dot(mask.astype(BF16), earlier, preferred_element_type=F32)
    return jnp.where(mask, rank, -1.0)


def block_kernel(tokens_ref, ids_ref, combine_ref, out_ref):
    tok = tokens_ref.shape[0]
    out_ref[:tok, :] = tokens_ref[...]
    parts = [ids_ref[...].astype(F32).astype(BF16)]
    left = combine_ref[...]
    for _ in range(3):
        part = left.astype(BF16)
        parts.append(part)
        left = left - part.astype(F32)
    out_ref[tok:, :] = jnp.concatenate(parts, axis=1)


def first_block(tokens, ids_t, combine_t):
    tok, width = tokens.shape
    return pl.pallas_call(
        block_kernel,
        out_shape=jax.ShapeDtypeStruct((tok + ids_t.shape[0], width), BF16),
        compiler_params=params(),
        name="first_block",
    )(tokens, ids_t, combine_t)


def dot(left, right):
    return jnp.dot(left, right, preferred_element_type=F32)


def contract_rows(left, right):
    return lax.dot_general(left, right, (((0,), (0,)), ((), ())), preferred_element_type=F32)


def on_device(tokens, out_grad, expert_ids, combine, w_gate, w_up, w_down):
    tok, top = expert_ids.shape
    n_y, n_z = lax.axis_size("y"), lax.axis_size("z")
    n_tp = lax.axis_size("tp")
    experts = n_y * n_z
    capacity = (tok * top * 9 + 8 * experts - 1) // (8 * experts)
    half = tokens.shape[1]
    columns = half // LANES
    group = 4
    groups = n_z // group
    rows = experts * capacity
    section = lax.axis_index("section")
    swap = [(0, 1), (1, 0)]

    grads_all = lax.all_gather(out_grad, "z", axis=0, tiled=True)

    both = jnp.concatenate([w_gate[0], w_up[0]], axis=1)
    hidden = w_gate.shape[2]
    down_t = w_down[0].T
    both_mine = lax.dynamic_slice_in_dim(both, section * half, half, 0)
    both_other = lax.dynamic_slice_in_dim(both, (1 - section) * half, half, 0)
    down_mine = lax.dynamic_slice_in_dim(down_t, section * half, half, 0)
    down_other = lax.dynamic_slice_in_dim(down_t, (1 - section) * half, half, 0)
    back_mine, back_other = both_mine.T, both_other.T

    ids_t, combine_t = expert_ids.T, combine.T

    ahead = [(c * n_z + i, c * n_z + (i + 1 - 2 * c) % n_z) for c in (0, 1) for i in range(n_z)]
    back = [(to, frm) for frm, to in ahead]
    ring = [None] * n_z
    ring[0] = low = high = first_block(tokens, ids_t, combine_t)
    for step in range(1, n_z // 2 + 1):
        low = lax.ppermute(low, ("section", "z"), ahead)
        ring[n_z - step] = low
        if step < n_z // 2:
            high = lax.ppermute(high, ("section", "z"), back)
            ring[step] = high

    spot = np.arange(rows)
    sub = (spot // capacity) % group
    of_y = (spot // (group * capacity)) % n_y
    source = of_y * n_z + spot // (n_y * group * capacity) * group + sub
    spread = (source[:, None] == np.arange(experts)[None, :]).astype(np.float32)
    spot = spot[: rows // groups]
    same = ((spot // capacity) % group)[:, None] == np.arange(group)[None, :]
    wanted = np.where(same, (spot % capacity)[:, None], -7).astype(np.float32)
    place = jnp.stack([lax.axis_index("z"), jnp.where(section == 0, 1, n_z - 1)])
    own_code = own_places(ids_t, experts)
    slots = np.arange(rows)
    unfold = (np.arange(experts)[:, None] == (slots // capacity)[None, :]).astype(np.float32)
    wide_own = contract_rows(own_code.astype(BF16), jnp.asarray(unfold, BF16))
    own_slot = jnp.asarray((slots % capacity).astype(np.float32))[None, :]
    unpick = (wide_own == own_slot).astype(BF16)

    send_rows, pick, scale = select_tokens(
        ring, place, jnp.asarray(spread, BF16), jnp.asarray(wanted), tok, n_y
    )
    send_rows, grads_all = lax.optimization_barrier((send_rows, grads_all))
    rows_mine = lax.all_to_all(send_rows, "y", 0, 0, tiled=True).reshape(rows, half)
    send_grads = select_grads(pick, grads_all, scale, n_y)
    rows_mine, send_grads = lax.optimization_barrier((rows_mine, send_grads))
    rows_other = lax.ppermute(rows_mine, "section", swap)
    grads_mine = lax.all_to_all(send_grads, "y", 0, 0, tiled=True).reshape(rows, half)
    grads_other = lax.ppermute(grads_mine, "section", swap)

    pre_part = (dot(rows_mine, both_mine) + dot(rows_other, both_other)).astype(BF16)
    hidden_part = (dot(grads_mine, down_mine) + dot(grads_other, down_other)).astype(BF16)
    pre = lax.psum_scatter(pre_part, "tp", scatter_dimension=0, tiled=True)
    hidden_terms = lax.all_to_all(
        hidden_part.reshape(n_tp, rows // n_tp, hidden), "tp", 0, 0, tiled=True
    )
    gate_pre, up_pre = pre[:, :hidden].astype(F32), pre[:, hidden:].astype(F32)
    hidden_grad = jnp.sum(hidden_terms.astype(F32), axis=0)
    sigmoid_g = jax.nn.sigmoid(gate_pre)
    activated = (gate_pre * sigmoid_g * up_pre).astype(BF16)
    gate_grad = hidden_grad * up_pre * sigmoid_g * (1.0 + gate_pre * (1.0 - sigmoid_g))
    up_grad = hidden_grad * gate_pre * sigmoid_g
    pre_grad = jnp.concatenate([gate_grad.astype(BF16), up_grad.astype(BF16)], axis=1)
    pre_grads = lax.all_to_all(
        jnp.broadcast_to(pre_grad[None], (n_tp,) + pre_grad.shape), "tp", 0, 0, tiled=True
    ).reshape(rows, 2 * hidden)
    activated_all = lax.all_gather(activated, "tp", axis=0, tiled=True)

    row_other = dot(pre_grads, back_other).astype(BF16)
    row_got = lax.ppermute(row_other, "section", swap)
    row_mine = dot(pre_grads, back_mine)
    packed = pack_rows(row_mine, row_got, capacity)
    returned = lax.all_to_all(
        packed.reshape(experts, columns * capacity, LANES), ("y", "z"), 0, 0, tiled=True
    )
    token_grad = combine_rows(unpick, returned.reshape(rows * columns, LANES), capacity)

    first = section == 0
    both_a = contract_rows(rows_mine, pre_grads).astype(BF16)
    both_b = contract_rows(rows_other, pre_grads).astype(BF16)
    down_a = contract_rows(activated_all, grads_mine).astype(BF16)
    down_b = contract_rows(activated_all, grads_other).astype(BF16)
    both_wgrad = jnp.concatenate(
        [jnp.where(first, both_a, both_b), jnp.where(first, both_b, both_a)], axis=0
    )
    down_wgrad = jnp.concatenate(
        [jnp.where(first, down_a, down_b), jnp.where(first, down_b, down_a)], axis=1
    )
    return (
        token_grad,
        both_wgrad[None, :, :hidden],
        both_wgrad[None, :, hidden:],
        down_wgrad[None],
    )


def solution(mesh):
    n_y = 4
    shape = mesh.shape
    fine = Mesh(
        mesh.devices.reshape(shape["section"], n_y, shape["expert"] // n_y, shape["tp"]),
        ("section", "y", "z", "tp"),
    )
    expert = ("y", "z")
    return jax.shard_map(
        on_device,
        mesh=fine,
        in_specs=(
            P(expert, ("tp", "section")),
            P(expert, ("tp", "section")),
            P(expert, None),
            P(expert, None),
            P(expert, "tp", "section"),
            P(expert, "tp", "section"),
            P(expert, "section", "tp"),
        ),
        out_specs=(
            P(expert, ("tp", "section")),
            P(expert, "tp", "section"),
            P(expert, "tp", "section"),
            P(expert, "section", "tp"),
        ),
        check_vma=False,
    )
```
